32 devices in a mesh: groups: 2 (over x), wide: 16 (over z, y, core).
Axes of the slice: x: 2, y: 2, z: 4, core: 2. Of those that a mesh axis runs over, the one named last changes fastest.
Arguments:
- prefix_hidden: bfloat16 [32, 256, 8192], P(('groups', 'wide')), parts along dimension 0, may hold values from -6 to 6
- prefix_lengths: int32 [32], P(('groups', 'wide')), parts along dimension 0, may hold values from 64 to 256
- action_noise: float32 [32, 50, 32], P(('groups', 'wide')), parts along dimension 0, may hold values from -4 to 4
- prefix_gain: float32 [8192], replicated, may hold values from 0.1 to 1.9
- key_weight: bfloat16 [8192, 512], P('wide'), may hold values from -0.0625 to 0.0625
- value_weight: bfloat16 [8192, 512], P('wide'), may hold values from -0.0625 to 0.0625
- input_weight: float32 [32, 1024], replicated, may hold values from -1 to 1
- expert_gain: float32 [1024], replicated, may hold values from 0.1 to 1.9
- expert_query: bfloat16 [1024, 1024], P('wide'), may hold values from -0.1875 to 0.1875
- expert_key: bfloat16 [1024, 512], P('wide'), may hold values from -5.3125 to 5.3125
- expert_value: bfloat16 [1024, 512], P('wide'), may hold values from -0.1875 to 0.1875
- expert_output: bfloat16 [1024, 1024], P('wide'), may hold values from -0.1875 to 0.1875
- final_gain: float32 [1024], replicated, may hold values from 0.1 to 1.9
- output_weight: bfloat16 [1024, 32], replicated, may hold values from -0.1875 to 0.1875
Outputs:
- actions: float32 [32, 50, 32], P(('groups', 'wide')), parts along dimension 0
The draws below stay inside these ranges and needn't reach their ends.
There are 2 independent parts, one for each index of `groups`. The reference program is written for one: setup_inputs(seed, part) draws one part's arguments, and reference() takes and returns one part's arrays. A program takes and returns all parts, laid end to end along the dimension named above; an argument that names none is the same for every part. Nothing has to cross between parts.
Inputs may be any that keep to these rules, and one draw needn't show every extreme that they name: `prefix_lengths`: positions at or after a sample's length are padding and take no part.
All inputs are finite; a program needn't handle non-finite values.
Results may differ from the reference program's by a relative error of at most 0.0075.
Values may be sent and summed in bfloat16 or wider, within the bound.
A program may use at most 128 MiB of HBM per device.

```python
import jax
import jax.numpy as jnp
from jax import lax

D = 8192
HEAD = 128
KV_HEADS = 4
ACT_WIDTH = 1024
ACT_HEADS = 8
ACT_DIM = 32
SPAN = 50
STEPS = 4
PREFIX = 256
SAMPLES = 16
KV = 512
QUERY_WIDTH = 1024


def coupled_weights(key):
    query_seed = jax.random.fold_in(key, 71)
    other_seed = jax.random.fold_in(key, 72)
    scale_factor = ACT_WIDTH ** (-0.5)
    query_draw = jnp.clip(jax.random.normal(query_seed, (ACT_WIDTH, ACT_HEADS * HEAD), jnp.float32), -6.0, 6.0) * scale_factor
    key_draw = jnp.clip(jax.random.normal(other_seed, (ACT_WIDTH, KV_HEADS * HEAD), jnp.float32), -6.0, 6.0) * scale_factor
    return (query_draw, key_draw)


def draw_expert_query(key, part):
    return coupled_weights(key)[0].astype(jnp.bfloat16)


def draw_expert_key(key, part):
    return coupled_weights(key)[1].astype(jnp.bfloat16)


def draw_action_noise(key, part):
    base_rows = jnp.clip(jax.random.normal(key, (SAMPLES, SPAN, ACT_DIM), jnp.float32), -4.0, 4.0)
    return base_rows


def touch_ends(array, rng, low, top_value):
    longest = array.shape.index(max(array.shape))
    spots = []
    for shift in (0, 1):
        where = [jax.random.randint(jax.random.fold_in(rng, axis), (), 0, length) for axis, length in enumerate(array.shape)]
        where[longest] = (where[longest] + shift) % array.shape[longest]
        spots.append(tuple(where))
    return array.at[spots[0]].set(low).at[spots[1]].set(top_value)


def levels(rng, dims, cuts, low, largest):
    level = 1.0
    for dim, parts in cuts:
        draws = jax.random.uniform(jax.random.fold_in(jax.random.fold_in(rng, 6), dim), (parts,), jnp.float32, low / len(cuts), largest / len(cuts))
        level = level * jnp.repeat(jnp.exp(draws), dims[dim] // parts).reshape((-1,) + (1,) * (len(dims) - 1 - dim))
    return level


def gaussian(key, shape, width, limit, pieces=(), kind=jnp.bfloat16):
    factor_of = levels(key, shape, pieces, -0.22, 0.18) if pieces else 1.0
    array = jax.random.normal(key, shape, jnp.float32) * width * factor_of
    return jnp.minimum(jnp.maximum(array, -limit), limit).astype(kind)


def setup_inputs(seed: int = 0, part: int = 0) -> dict:
    seeds = jax.random.split(jax.random.key(seed), 15)
    part_keys = jax.random.split(jax.random.fold_in(seeds[14], part), 15)
    return {
        "prefix_hidden": gaussian(part_keys[0], (SAMPLES, PREFIX, D), 1.0, 6.0, ((0, 16),)),
        "prefix_lengths": touch_ends(jax.random.randint(part_keys[1], (SAMPLES,), PREFIX // 4, PREFIX + 1), jax.random.fold_in(part_keys[1], 1), PREFIX // 4, PREFIX).astype(jnp.int32),
        "action_noise": draw_action_noise(jax.random.fold_in(jax.random.fold_in(seeds[14], part), 71), part),
        "prefix_gain": jnp.clip(1.0 + 0.18 * jax.random.normal(seeds[3], (D,), jnp.float32), 0.1, 1.9),
        "key_weight": gaussian(seeds[4], (D, KV), D ** -0.5, 0.0625, ((0, 16),)),
        "value_weight": gaussian(seeds[5], (D, KV), D ** -0.5, 0.0625, ((0, 16),)),
        "input_weight": gaussian(seeds[6], (ACT_DIM, ACT_WIDTH), ACT_DIM ** -0.5, 1.0, (), jnp.float32),
        "expert_gain": jnp.clip(1.0 + 0.18 * jax.random.normal(seeds[7], (ACT_WIDTH,), jnp.float32), 0.1, 1.9),
        "expert_query": draw_expert_query(jax.random.fold_in(seeds[14], 71), part),
        "expert_key": draw_expert_key(jax.random.fold_in(seeds[14], 71), part),
        "expert_value": gaussian(seeds[10], (ACT_WIDTH, KV), ACT_WIDTH ** -0.5, 0.1875, ((0, 16),)),
        "expert_output": gaussian(seeds[11], (QUERY_WIDTH, ACT_WIDTH), QUERY_WIDTH ** -0.5, 0.1875, ((0, 16),)),
        "final_gain": jnp.clip(1.0 + 0.18 * jax.random.normal(seeds[12], (ACT_WIDTH,), jnp.float32), 0.1, 1.9),
        "output_weight": gaussian(seeds[13], (ACT_WIDTH, ACT_DIM), ACT_WIDTH ** -0.5, 0.1875),
    }


rope_base = 1000000.0
norm_eps = 1e-06

def normalize(values, norm_gain):
    mean_square = lax.optimization_barrier(jnp.mean(values * values, axis=-1, keepdims=True))
    return values * lax.rsqrt(mean_square + norm_eps) * norm_gain

def rotate(values, positions):
    half_width = values.shape[-1] // 2
    inv_freqs = rope_base ** (-jnp.arange(half_width, dtype=jnp.float32) * 2.0 / values.shape[-1])
    angles = positions[:, None] * inv_freqs[None, :]
    cosine = jnp.cos(angles)[:, None, :]
    sine_part = jnp.sin(angles)[:, None, :]
    first_half = values[..., :half_width]
    second = values[..., half_width:]
    return jnp.concatenate([first_half * cosine - second * sine_part, second * cosine + first_half * sine_part], -1)

def time_embedding(time_value, embed_width):
    half_width = embed_width // 2
    fraction = jnp.arange(half_width, dtype=jnp.float32) / (half_width - 1)
    period = 0.004 * (4.0 / 0.004) ** fraction
    angles = time_value * (2.0 * jnp.pi) / period
    return jnp.concatenate([jnp.sin(angles), jnp.cos(angles)])

def attend(queries, key_cache, value_cache, action_keys, action_values, is_valid):
    span_rows = queries.shape[0]
    groups = key_cache.shape[1] // HEAD
    group_ratio = queries.shape[1] // key_cache.shape[1]
    query_heads = queries.reshape(span_rows, groups, group_ratio, HEAD).astype(jnp.float32)
    prefix_keys = key_cache.reshape(-1, groups, HEAD).astype(jnp.float32)
    prefix_values = value_cache.reshape(-1, groups, HEAD).astype(jnp.float32)
    own_keys = action_keys.reshape(span_rows, groups, HEAD).astype(jnp.float32)
    own_values = action_values.reshape(span_rows, groups, HEAD).astype(jnp.float32)
    prefix_scores = jnp.einsum('cgrh,pgh->grcp', query_heads, prefix_keys)
    prefix_scores = jnp.where(is_valid[None, None, None, :], prefix_scores, -1e+30)
    own_scores = jnp.einsum('cgrh,ngh->grcn', query_heads, own_keys)
    row_max = jnp.maximum(lax.optimization_barrier(jnp.max(prefix_scores, -1)), lax.optimization_barrier(jnp.max(own_scores, -1)))[..., None]
    prefix_exp = jnp.exp(prefix_scores - row_max)
    own_exp = jnp.exp(own_scores - row_max)
    prob_total = lax.optimization_barrier(jnp.sum(prefix_exp, -1, keepdims=True)) + lax.optimization_barrier(jnp.sum(own_exp, -1, keepdims=True))
    prefix_prob = (prefix_exp / prob_total).astype(jnp.bfloat16).astype(jnp.float32)
    own_prob = (own_exp / prob_total).astype(jnp.bfloat16).astype(jnp.float32)
    attn_mixed = jnp.einsum('grcp,pgh->cgrh', prefix_prob, prefix_values) + jnp.einsum('grcn,ngh->cgrh', own_prob, own_values)
    return attn_mixed.reshape(span_rows, -1).astype(jnp.bfloat16)

def prefill_one(hidden, prefix_gain, key_weight, value_weight):
    row_count = hidden.shape[0]
    normed = normalize(hidden.astype(jnp.float32), prefix_gain).astype(jnp.bfloat16)
    raw_keys = jnp.dot(normed, key_weight, preferred_element_type=jnp.float32)
    raw_values = jnp.dot(normed, value_weight, preferred_element_type=jnp.float32)
    positions = jnp.arange(row_count, dtype=jnp.float32)
    key_cache = rotate(raw_keys.reshape(row_count, -1, HEAD), positions).reshape(row_count, -1).astype(jnp.bfloat16)
    return (key_cache, raw_values.astype(jnp.bfloat16))

def expert_steps(noise_rows, length, input_weight, expert_gain, query_w, key_w, value_w, output_w, final_gain, output_weight, key_cache, value_cache):
    span_rows = noise_rows.shape[0]
    is_valid = jnp.arange(key_cache.shape[0], dtype=jnp.int32) < length
    positions = length.astype(jnp.float32) + jnp.arange(span_rows, dtype=jnp.float32)
    action_state = noise_rows
    for step_idx in range(STEPS):
        time_value = 1.0 - step_idx / STEPS
        hidden = jnp.dot(action_state, input_weight, precision=lax.Precision.HIGHEST, preferred_element_type=jnp.float32)
        hidden = hidden + time_embedding(time_value, input_weight.shape[1])[None, :]
        normed = normalize(hidden, expert_gain).astype(jnp.bfloat16)
        raw_queries = jnp.dot(normed, query_w, preferred_element_type=jnp.float32)
        queries = rotate(raw_queries.reshape(span_rows, -1, HEAD), positions).reshape(span_rows, -1)
        queries = (queries * HEAD ** (-0.5)).astype(jnp.bfloat16)
        raw_keys = jnp.dot(normed, key_w, preferred_element_type=jnp.float32)
        action_keys = rotate(raw_keys.reshape(span_rows, -1, HEAD), positions).reshape(span_rows, -1).astype(jnp.bfloat16)
        action_values = jnp.dot(normed, value_w, preferred_element_type=jnp.float32).astype(jnp.bfloat16)
        attn_mixed = attend(queries, key_cache, value_cache, action_keys, action_values, is_valid)
        hidden = hidden + jnp.dot(attn_mixed, output_w, preferred_element_type=jnp.float32)
        final_normed = normalize(hidden, final_gain).astype(jnp.bfloat16)
        velocity = jnp.dot(final_normed, output_weight, preferred_element_type=jnp.float32)
        action_state = action_state - velocity / STEPS
    return action_state

def reference(prefix_hidden, prefix_lengths, action_noise, prefix_gain, key_weight, value_weight, input_weight, expert_gain, expert_query, expert_key, expert_value, expert_output, final_gain, output_weight):

    def one_sample(sample_args):
        hidden, length, noise_rows = sample_args
        key_cache, value_cache = prefill_one(hidden, prefix_gain, key_weight, value_weight)
        return expert_steps(noise_rows, length, input_weight, expert_gain, expert_query, expert_key, expert_value, expert_output, final_gain, output_weight, key_cache, value_cache)
    return lax.map(one_sample, (prefix_hidden, prefix_lengths, action_noise))
```

```python
import functools

import jax
import jax.numpy as jnp
import numpy as np
from jax import lax
from jax.experimental import pallas as pl
from jax.experimental.pallas import tpu as pltpu
from jax.sharding import PartitionSpec as P

HEAD = 128
STEPS = 4
ROWS = 64

rope_base = 1000000.0
norm_eps = 1e-06


def rope_tables(rows):
    half = HEAD // 2
    inv = (np.float32(rope_base) ** (-np.arange(half, dtype=np.float32) * np.float32(2.0) / np.float32(HEAD))).astype(np.float32)
    angles = np.arange(rows, dtype=np.float32)[:, None] * inv[None, :]
    cosine, sine = np.cos(angles), np.sin(angles)
    return (
        np.concatenate([cosine, cosine], 1).astype(np.float32),
        np.concatenate([-sine, sine], 1).astype(np.float32),
    )


def time_embeddings(width):
    half = width // 2
    fraction = np.arange(half, dtype=np.float32) / np.float32(half - 1)
    period = np.float32(0.004) * np.float32(4.0 / 0.004) ** fraction
    rows = []
    for k in range(STEPS):
        angles = np.float32((1.0 - k / STEPS) * 2.0 * np.pi) / period
        rows.append(np.concatenate([np.sin(angles), np.cos(angles)]))
    return np.stack(rows).astype(np.float32)


def normalize(values, gain):
    mean_square = jnp.mean(values * values, axis=-1, keepdims=True)
    return values * lax.rsqrt(mean_square + norm_eps) * gain


def rotate(values, cosine, sine):
    return values * cosine + pltpu.roll(values, HEAD // 2, 1) * sine


def gather_kernel(
    nz, ny,
    key_ref, value_ref, query_ref, akey_ref, avalue_ref, out_ref, hidden_ref, gain_ref, cos_ref, sin_ref,
    k_out, v_out, e_out,
    buf, hid, normed, acc,
    own_sem, hid_sem, recv, zsend, ysend, xsend, csend, esem,
):
    kv_rows, kv = key_ref.shape
    e_rows, total = query_ref.shape[0], buf.shape[1]
    r1 = (total * 11 // 32 + 8) // 16 * 16
    r0 = total - 2 * r1
    g, w = lax.axis_index("groups"), lax.axis_index("wide")
    c, y, z = w % 2, (w // 2) % ny, w // (2 * ny)
    parity = g % 2

    def shard(zz, other_y, cc):
        yy = 1 - y if other_y else y
        return (zz * ny + yy) * 2 + cc

    def piece(k):
        if k == 0:
            return 0, r0, 0
        which = parity if k == 1 else 1 - parity
        return pl.multiple_of(r0 + which * r1, 16), r1, 1 + which

    core = {"wide": w + 1 - 2 * c}
    across = {"groups": g + 1 - 2 * parity}
    beside = {"wide": w + 2 - 4 * y} if ny > 1 else None

    def move(s, k, send, target):
        start, size, a = piece(k)
        part = buf.at[s, pl.ds(start, size), :]
        return pltpu.make_async_remote_copy(
            src_ref=part, dst_ref=part, send_sem=send, recv_sem=recv.at[s, a],
            device_id=target, device_id_type=pl.DeviceIdType.MESH,
        )

    def arrived(s, k):
        move(s, k, csend.at[0, 0], core).wait_recv()

    up, down = z + 1 < nz, z > 0

    def z_move(d, zz, k):
        return move(shard(zz, False, c), k, zsend.at[(d + 1) // 2, zz, k], {"wide": w + d * 2 * ny})

    def y_move(zz, k):
        return move(shard(zz, False, c), k, ysend.at[zz, k], beside)

    def x_move(zz, other_y):
        return move(shard(zz, other_y, c), 1, xsend.at[int(other_y), zz], across)

    def c_move(zz, other_y, k):
        return move(shard(zz, other_y, c), k, csend.at[int(other_y) * nz + zz, k], core)

    own = [
        (key_ref, buf.at[w, 0:kv_rows, 0:kv]),
        (value_ref, buf.at[w, 0:kv_rows, kv:2 * kv]),
        (query_ref, buf.at[w, kv_rows:kv_rows + e_rows, :]),
        (akey_ref, buf.at[w, kv_rows + e_rows:kv_rows + 2 * e_rows, 0:kv]),
        (avalue_ref, buf.at[w, kv_rows + e_rows:kv_rows + 2 * e_rows, kv:2 * kv]),
        (out_ref, buf.at[w, kv_rows + 2 * e_rows:total, :]),
    ]
    copies = [pltpu.make_async_copy(a, b, own_sem.at[i]) for i, (a, b) in enumerate(own)]
    for copy in copies:
        copy.start()
    hid_copy = pltpu.make_async_copy(hidden_ref.at[0], hid, hid_sem)
    hid_copy.start()

    barrier = pltpu.get_barrier_semaphore()

    def greet(target):
        pl.semaphore_signal(barrier, inc=1, device_id=target, device_id_type=pl.DeviceIdType.MESH)

    greet(core)
    greet(across)
    if ny > 1:
        greet(beside)

    @pl.when(up)
    def _():
        greet({"wide": w + 2 * ny})

    @pl.when(down)
    def _():
        greet({"wide": w - 2 * ny})

    pl.semaphore_wait(barrier, 2 + (ny > 1) + up.astype(jnp.int32) + down.astype(jnp.int32))
    for copy in copies:
        copy.wait()

    for k in (1, 0):
        @pl.when(up)
        def _():
            z_move(1, z, k).start()

        @pl.when(down)
        def _():
            z_move(-1, z, k).start()

        if ny > 1:
            y_move(z, k).start()
    for k in (1, 0, 2):
        c_move(z, False, k).start()

    hid_copy.wait()
    width = hid.shape[1]
    squares = jnp.zeros((hid.shape[0], HEAD), jnp.float32)

    def square(j, squares):
        part = hid[:, pl.ds(pl.multiple_of(j * HEAD, HEAD), HEAD)].astype(jnp.float32)
        return squares + part * part

    squares = lax.fori_loop(0, width // HEAD, square, squares)
    scale = lax.rsqrt(jnp.sum(squares, -1, keepdims=True) / width + norm_eps)
    wide_scale = jnp.broadcast_to(scale, (hid.shape[0], HEAD))
    per = kv_rows // HEAD

    def norm_part(j, carry):
        for i in range(per):
            at = pl.ds(pl.multiple_of((j * per + i) * HEAD, HEAD), HEAD)
            part = hid[:, at].astype(jnp.float32) * wide_scale * gain_ref[:, at]
            normed[j, :, i * HEAD:(i + 1) * HEAD] = part.astype(jnp.bfloat16)
        return carry

    lax.fori_loop(0, width // kv_rows, norm_part, 0)
    acc[...] = jnp.zeros_like(acc)

    def blocks(t, first, body):
        for d in (1, -1):
            zz = z - d * t
            ok = (zz >= 0) & (zz < nz) & (t >= first) & (t < nz)
            if d == -1:
                ok = ok & (t > 0)

            @pl.when(ok)
            def _():
                body(d, zz)

    def step(i, carry):
        for k in (1, 0):
            def line(d, zz, k=k):
                arrived(shard(zz, False, c), k)

                @pl.when((z + d >= 0) & (z + d < nz))
                def _():
                    z_move(d, zz, k).start()

                if ny > 1:
                    y_move(zz, k).start()
                if k == 1:
                    x_move(zz, False).start()
                c_move(zz, False, k).start()

            blocks(i, 1, line)
        if ny > 1:
            for k in (1, 0):
                def side(d, zz, k=k):
                    arrived(shard(zz, True, c), k)
                    if k == 1:
                        x_move(zz, True).start()
                    c_move(zz, True, k).start()

                blocks(i - 1, 0, side)
        for other_y in ((False, True) if ny > 1 else (False,)):
            def over(d, zz, other_y=other_y):
                arrived(shard(zz, other_y, c), 2)
                c_move(zz, other_y, 2).start()

            blocks(i - 2, 0 if other_y else 1, over)

        t = i - 3

        def use(q, carry):
            mine, yy, back = q % 2, (q // 2) % ny, q // (2 * ny)
            zz = z - t + back * 2 * t
            s = (zz * ny + (y + yy) % ny) * 2 + (c + mine) % 2

            @pl.when((zz >= 0) & (zz < nz) & (t >= 0) & ((back == 0) | (t > 0)))
            def _():
                @pl.when(mine == 1)
                def _():
                    for k in (1, 0, 2):
                        arrived(s, k)

                pltpu.make_async_copy(buf.at[s, kv_rows:total, :], e_out.at[s], esem.at[s]).start()
                acc[...] += jnp.dot(normed[s], buf[s, 0:kv_rows, :], preferred_element_type=jnp.float32)

            return carry

        return lax.fori_loop(0, 4 * ny, use, carry)

    lax.fori_loop(0, nz + 3, step, 0)

    rows = acc.shape[0]
    for h in range(kv // HEAD):
        at = slice(h * HEAD, (h + 1) * HEAD)
        k_out[:, at] = rotate(acc[:, at], cos_ref[...], sin_ref[...]).astype(jnp.bfloat16)
    v_out[...] = acc[:, kv:2 * kv].astype(jnp.bfloat16)

    def finish(t, carry):
        def line(d, zz):
            if ny > 1:
                for k in (1, 0):
                    y_move(zz, k).wait_send()

            @pl.when(t > 0)
            def _():
                x_move(zz, False).wait_send()

            for k in (1, 0, 2):
                c_move(zz, False, k).wait_send()
            if ny > 1:
                x_move(zz, True).wait_send()
                for k in (1, 0, 2):
                    c_move(zz, True, k).wait_send()

        def forward(d, zz):
            @pl.when((z + d >= 0) & (z + d < nz))
            def _():
                for k in (1, 0):
                    z_move(d, zz, k).wait_send()

        blocks(t, 0, line)
        blocks(t, 1, forward)
        return carry

    for k in (1, 0):
        @pl.when(up)
        def _():
            z_move(1, z, k).wait_send()

        @pl.when(down)
        def _():
            z_move(-1, z, k).wait_send()

    lax.fori_loop(0, nz, finish, 0)

    def drain(s, carry):
        pltpu.make_async_copy(buf.at[s, kv_rows:total, :], e_out.at[s], esem.at[s]).wait()
        return carry

    lax.fori_loop(0, buf.shape[0], drain, 0)


def steps_kernel(
    length_ref, noise_ref, input_ref, temb_ref, gain_ref, e_ref, final_ref, outw_ref, k_ref, v_ref, cos_ref, sin_ref,
    o_ref, state, keys, values, mixed,
):
    n, e3, width = e_ref.shape
    e_rows = e3 // 3
    span = noise_ref.shape[1]
    prefix, kv = k_ref.shape
    heads, kv_heads = width // HEAD, kv // HEAD
    ratio = heads // kv_heads
    length = length_ref[0]
    state[...] = jnp.zeros_like(state)
    state[0:span, :] = noise_ref[0]
    keys[0:prefix, :] = k_ref[...]
    values[0:prefix, :] = v_ref[...]
    cosine = cos_ref[pl.ds(length, ROWS), :]
    sine = sin_ref[pl.ds(length, ROWS), :]
    at = lax.broadcasted_iota(jnp.int32, (ratio * ROWS, prefix + ROWS), 1)
    valid = (at < length) | ((at >= prefix) & (at < prefix + span))

    def weight(i):
        return e_ref[:, i * e_rows:(i + 1) * e_rows, :].reshape(n * e_rows, width)

    def step(k, carry):
        hidden = jnp.dot(state[...], input_ref[...], precision=lax.Precision.HIGHEST, preferred_element_type=jnp.float32)
        hidden = hidden + temb_ref[pl.ds(k, 1), :]
        normed = normalize(hidden, gain_ref[...]).astype(jnp.bfloat16)
        raw = jnp.dot(normed, weight(1), preferred_element_type=jnp.float32)
        for h in range(kv_heads):
            cut = slice(h * HEAD, (h + 1) * HEAD)
            keys[prefix:, cut] = rotate(raw[:, cut], cosine, sine).astype(jnp.bfloat16)
        values[prefix:, :] = raw[:, kv:].astype(jnp.bfloat16)
        raw = jnp.dot(normed, weight(0), preferred_element_type=jnp.float32)
        for h in range(kv_heads):
            cut = slice(h * HEAD, (h + 1) * HEAD)
            queries = jnp.concatenate(
                [
                    (rotate(raw[:, j * HEAD:(j + 1) * HEAD], cosine, sine) * HEAD ** (-0.5)).astype(jnp.bfloat16)
                    for j in range(h * ratio, (h + 1) * ratio)
                ],
                0,
            )
            scores = lax.dot_general(queries, keys[:, cut], (((1,), (1,)), ((), ())), preferred_element_type=jnp.float32)
            scores = jnp.where(valid, scores, -1e30)
            weights = jnp.exp(scores - jnp.max(scores, -1, keepdims=True))
            probs = (weights / jnp.sum(weights, -1, keepdims=True)).astype(jnp.bfloat16)
            out = jnp.dot(probs, values[:, cut], preferred_element_type=jnp.float32).astype(jnp.bfloat16)
            for j in range(ratio):
                mixed[:, (h * ratio + j) * HEAD:(h * ratio + j + 1) * HEAD] = out[j * ROWS:(j + 1) * ROWS]
        hidden = hidden + jnp.dot(mixed[...], weight(2), preferred_element_type=jnp.float32)
        normed = normalize(hidden, final_ref[...]).astype(jnp.bfloat16)
        velocity = jnp.dot(normed, outw_ref[...], preferred_element_type=jnp.float32)
        state[...] = state[...] - velocity / STEPS
        return carry

    lax.fori_loop(0, STEPS, step, 0)
    o_ref[0] = state[0:span, :]


def shards(
    nz, ny,
    prefix_hidden, prefix_lengths, action_noise, prefix_gain, key_weight, value_weight, input_weight, expert_gain,
    expert_query, expert_key, expert_value, expert_output, final_gain, output_weight,
):
    n = nz * ny * 2
    prefix, width = prefix_hidden.shape[1:]
    kv_rows, kv = key_weight.shape
    e_rows, e_width = expert_query.shape
    total = kv_rows + 3 * e_rows
    span, dim = action_noise.shape[1:]
    cosine, sine = rope_tables(prefix + ROWS + 8)
    vmem, hbm = pl.BlockSpec(memory_space=pltpu.VMEM), pl.BlockSpec(memory_space=pl.ANY)
    bf16, f32 = jnp.bfloat16, jnp.float32
    dma = pltpu.SemaphoreType.DMA
    k_cache, v_cache, expert = pl.pallas_call(
        functools.partial(gather_kernel, nz, ny),
        out_shape=(
            jax.ShapeDtypeStruct((prefix, kv), bf16),
            jax.ShapeDtypeStruct((prefix, kv), bf16),
            jax.ShapeDtypeStruct((n, 3 * e_rows, e_width), bf16),
        ),
        in_specs=[hbm] * 7 + [vmem] * 3,
        out_specs=(vmem, vmem, hbm),
        scratch_shapes=[
            pltpu.VMEM((n, total, 2 * kv), bf16),
            pltpu.VMEM((prefix, width), bf16),
            pltpu.VMEM((n, prefix, kv_rows), bf16),
            pltpu.VMEM((prefix, 2 * kv), f32),
            dma((6,)),
            dma,
            dma((n, 3)),
            dma((2, nz, 2)),
            dma((nz, 2)),
            dma((2, nz)),
            dma((ny * nz, 3)),
            dma((n,)),
        ],
        compiler_params=pltpu.CompilerParams(collective_id=0, has_side_effects=True, vmem_limit_bytes=60 * 2 ** 20),
        name="gather",
    )(
        key_weight, value_weight, expert_query, expert_key, expert_value, expert_output,
        prefix_hidden, prefix_gain.reshape(1, -1), jnp.asarray(cosine[:prefix]), jnp.asarray(sine[:prefix]),
    )
    return pl.pallas_call(
        steps_kernel,
        out_shape=jax.ShapeDtypeStruct((1, span, dim), f32),
        in_specs=[pl.BlockSpec(memory_space=pltpu.SMEM)] + [vmem] * 11,
        out_specs=vmem,
        scratch_shapes=[
            pltpu.VMEM((ROWS, dim), f32),
            pltpu.VMEM((prefix + ROWS, kv), bf16),
            pltpu.VMEM((prefix + ROWS, kv), bf16),
            pltpu.VMEM((ROWS, e_width), bf16),
        ],
        name="steps",
    )(
        prefix_lengths, action_noise, input_weight, jnp.asarray(time_embeddings(e_width)), expert_gain.reshape(1, -1),
        expert, final_gain.reshape(1, -1), output_weight, k_cache, v_cache, jnp.asarray(cosine), jnp.asarray(sine),
    )


def solution(mesh):
    n = mesh.shape["wide"]
    column = mesh.devices[0] if mesh.axis_names[0] == "groups" else mesh.devices[:, 0]
    ny = len({d.coords[1] for d in column.flat}) if all(hasattr(d, "coords") for d in column.flat) else 1
    nz = n // (2 * ny)
    placed = (
        P(("groups", "wide"), None, None),
        P(("groups", "wide")),
        P(("groups", "wide"), None, None),
        P(),
        P("wide", None),
        P("wide", None),
        P(),
        P(),
        P("wide", None),
        P("wide", None),
        P("wide", None),
        P("wide", None),
        P(),
        P(),
    )
    return jax.shard_map(
        functools.partial(shards, nz, ny),
        mesh=mesh,
        in_specs=placed,
        out_specs=P(("groups", "wide"), None, None),
        check_vma=False,
    )
```

```python
import functools

import jax
import jax.numpy as jnp
import numpy as np
from jax import lax
from jax.experimental import pallas as pl
from jax.experimental.pallas import tpu as pltpu
from jax.sharding import PartitionSpec as P

HEAD = 128
STEPS = 4
ROWS = 64

rope_base = 1000000.0
norm_eps = 1e-06


def rope_tables(rows):
    half = HEAD // 2
    inv = (np.float32(rope_base) ** (-np.arange(half, dtype=np.float32) * np.float32(2.0) / np.float32(HEAD))).astype(np.float32)
    angles = np.arange(rows, dtype=np.float32)[:, None] * inv[None, :]
    cosine, sine = np.cos(angles), np.sin(angles)
    return (
        np.concatenate([cosine, cosine], 1).astype(np.float32),
        np.concatenate([-sine, sine], 1).astype(np.float32),
    )


def time_embeddings(width):
    half = width // 2
    fraction = np.arange(half, dtype=np.float32) / np.float32(half - 1)
    period = np.float32(0.004) * np.float32(4.0 / 0.004) ** fraction
    rows = []
    for k in range(STEPS):
        angles = np.float32((1.0 - k / STEPS) * 2.0 * np.pi) / period
        rows.append(np.concatenate([np.sin(angles), np.cos(angles)]))
    return np.stack(rows).astype(np.float32)


def normalize(values, gain):
    mean_square = jnp.mean(values * values, axis=-1, keepdims=True)
    return values * lax.rsqrt(mean_square + norm_eps) * gain


def rotate(values, cosine, sine):
    return values * cosine + pltpu.roll(values, HEAD // 2, 1) * sine


def share(total, ny):
    if ny == 1:
        return (total * 11 // 32 + 8) // 16 * 16, 0
    return (total * 13 // 44 + 8) // 16 * 16, (total * 3 // 22 + 8) // 16 * 16


def gather_kernel(
    nz, ny,
    key_ref, value_ref, query_ref, akey_ref, avalue_ref, out_ref, hidden_ref, gain_ref, cos_ref, sin_ref,
    k_out, v_out, e_out,
    buf, hid, normed, acc,
    own_sem, hid_sem, recv, zsend, ysend, xsend, csend, esem,
):
    kv_rows, kv = key_ref.shape
    e_rows, total = query_ref.shape[0], buf.shape[1]
    r1, rb = share(total, ny)
    r0 = total - 2 * r1 - rb
    g, w = lax.axis_index("groups"), lax.axis_index("wide")
    c, y, z = w % 2, (w // 2) % ny, w // (2 * ny)
    parity = g % 2

    def shard(zz, other_y, cc):
        yy = 1 - y if other_y else y
        return (zz * ny + yy) * 2 + cc

    def piece(k):
        if k == 0:
            return 0, r0, 0
        if k == 3:
            return r0, rb, 3
        which = parity if k == 1 else 1 - parity
        return pl.multiple_of(r0 + rb + which * r1, 16), r1, 1 + which

    core = {"wide": w + 1 - 2 * c}
    across = {"groups": g + 1 - 2 * parity}
    beside = {"wide": w + 2 - 4 * y} if ny > 1 else None

    def move(s, k, send, target):
        start, size, a = piece(k)
        part = buf.at[s, pl.ds(start, size), :]
        return pltpu.make_async_remote_copy(
            src_ref=part, dst_ref=part, send_sem=send, recv_sem=recv.at[s, a],
            device_id=target, device_id_type=pl.DeviceIdType.MESH,
        )

    def arrived(s, k):
        move(s, k, csend.at[0, 0], core).wait_recv()

    up, down = z + 1 < nz, z > 0
    every = (1, 0, 2, 3) if ny > 1 else (1, 0, 2)

    def z_move(d, zz, k):
        return move(shard(zz, False, c), k, zsend.at[(d + 1) // 2, zz, k], {"wide": w + d * 2 * ny})

    def b_move(d, zz, other_y):
        return move(shard(zz, other_y, c), 3, zsend.at[(d + 1) // 2, zz, 2 + other_y], {"wide": w + d * 2 * ny})

    def y_move(zz, k):
        return move(shard(zz, False, c), k, ysend.at[zz, min(k, 2)], beside)

    def x_move(zz, other_y):
        return move(shard(zz, other_y, c), 1, xsend.at[int(other_y), zz], across)

    def c_move(zz, other_y, k):
        return move(shard(zz, other_y, c), k, csend.at[int(other_y) * nz + zz, k], core)

    own = [
        (key_ref, buf.at[w, 0:kv_rows, 0:kv]),
        (value_ref, buf.at[w, 0:kv_rows, kv:2 * kv]),
        (query_ref, buf.at[w, kv_rows:kv_rows + e_rows, :]),
        (akey_ref, buf.at[w, kv_rows + e_rows:kv_rows + 2 * e_rows, 0:kv]),
        (avalue_ref, buf.at[w, kv_rows + e_rows:kv_rows + 2 * e_rows, kv:2 * kv]),
        (out_ref, buf.at[w, kv_rows + 2 * e_rows:total, :]),
    ]
    copies = [pltpu.make_async_copy(a, b, own_sem.at[i]) for i, (a, b) in enumerate(own)]
    for copy in copies:
        copy.start()
    hid_copy = pltpu.make_async_copy(hidden_ref.at[0], hid, hid_sem)
    hid_copy.start()

    barrier = pltpu.get_barrier_semaphore()

    def greet(target):
        pl.semaphore_signal(barrier, inc=1, device_id=target, device_id_type=pl.DeviceIdType.MESH)

    greet(core)
    greet(across)
    if ny > 1:
        greet(beside)

    @pl.when(up)
    def _():
        greet({"wide": w + 2 * ny})

    @pl.when(down)
    def _():
        greet({"wide": w - 2 * ny})

    pl.semaphore_wait(barrier, 2 + (ny > 1) + up.astype(jnp.int32) + down.astype(jnp.int32))
    for copy in copies:
        copy.wait()

    for k in (1, 0):
        @pl.when(up)
        def _():
            z_move(1, z, k).start()

        @pl.when(down)
        def _():
            z_move(-1, z, k).start()

        if ny > 1:
            y_move(z, k).start()
    if ny > 1:
        y_move(z, 3).start()
    for k in every:
        c_move(z, False, k).start()

    hid_copy.wait()
    width = hid.shape[1]
    squares = jnp.zeros((hid.shape[0], HEAD), jnp.float32)

    def square(j, squares):
        part = hid[:, pl.ds(pl.multiple_of(j * HEAD, HEAD), HEAD)].astype(jnp.float32)
        return squares + part * part

    squares = lax.fori_loop(0, width // HEAD, square, squares)
    scale = lax.rsqrt(jnp.sum(squares, -1, keepdims=True) / width + norm_eps)
    wide_scale = jnp.broadcast_to(scale, (hid.shape[0], HEAD))
    per = kv_rows // HEAD

    def norm_part(j, carry):
        for i in range(per):
            at = pl.ds(pl.multiple_of((j * per + i) * HEAD, HEAD), HEAD)
            part = hid[:, at].astype(jnp.float32) * wide_scale * gain_ref[:, at]
            normed[j, :, i * HEAD:(i + 1) * HEAD] = part.astype(jnp.bfloat16)
        return carry

    lax.fori_loop(0, width // kv_rows, norm_part, 0)
    acc[...] = jnp.zeros_like(acc)

    def blocks(t, first, body):
        for d in (1, -1):
            zz = z - d * t
            ok = (zz >= 0) & (zz < nz) & (t >= first) & (t < nz)
            if d == -1:
                ok = ok & (t > 0)

            @pl.when(ok)
            def _():
                body(d, zz)

    def slot(j, first, body):
        paired = jnp.minimum(z, nz - 1 - z)
        t = jnp.where(j <= 2 * paired, (j + 1) // 2, j - paired)
        below = jnp.where(j <= 2 * paired, j % 2, (z > nz - 1 - z).astype(jnp.int32))
        zz = z + t - 2 * below * t

        @pl.when((j >= first) & (j < nz))
        def _():
            body(zz)

    def step(i, carry):
        for k in (1, 0):
            def line(d, zz, k=k):
                arrived(shard(zz, False, c), k)

                @pl.when((z + d >= 0) & (z + d < nz))
                def _():
                    z_move(d, zz, k).start()

                if k == 1:
                    x_move(zz, False).start()
                if ny > 1:
                    if d == 1:
                        y_move(zz, k).start()
                    else:
                        @pl.when((z - i >= 0) == (k == 0))
                        def _():
                            y_move(zz, 1).start()

                        if k == 0:
                            y_move(zz, 0).start()
                c_move(zz, False, k).start()

            blocks(i, 1, line)
        def side(k):
            def body(zz):
                arrived(shard(zz, True, c), k)
                if k == 1:
                    x_move(zz, True).start()
                c_move(zz, True, k).start()

            slot(i - 1, 0, body)

        def both(d, zz):
            for other_y in (False, True):
                arrived(shard(zz, other_y, c), 3)

                @pl.when((z + d >= 0) & (z + d < nz))
                def _():
                    b_move(d, zz, other_y).start()

                c_move(zz, other_y, 3).start()

        if ny > 1:
            side(1)

            @pl.when(i == 2)
            def _():
                arrived(shard(z, True, c), 3)
                for other_y in (False, True):
                    @pl.when(up)
                    def _():
                        b_move(1, z, other_y).start()

                    @pl.when(down)
                    def _():
                        b_move(-1, z, other_y).start()

                c_move(z, True, 3).start()

            blocks(i - 2, 1, both)
            side(0)
        for other_y in ((False, True) if ny > 1 else (False,)):
            def over(zz, other_y=other_y):
                arrived(shard(zz, other_y, c), 2)
                c_move(zz, other_y, 2).start()

            slot(i - 2, 0 if other_y else 1, over)

        def pair(zz):
            def use(q, carry):
                mine, yy = q % 2, q // 2
                s = (zz * ny + (y + yy) % ny) * 2 + (c + mine) % 2

                @pl.when(mine == 1)
                def _():
                    for k in every:
                        arrived(s, k)

                pltpu.make_async_copy(buf.at[s, kv_rows:total, :], e_out.at[s], esem.at[s]).start()
                acc[...] += jnp.dot(normed[s], buf[s, 0:kv_rows, :], preferred_element_type=jnp.float32)
                return carry

            lax.fori_loop(0, 2 * ny, use, 0)

        slot(i - 3, 0, pair)
        return carry

    lax.fori_loop(0, nz + 3, step, 0)

    rows = acc.shape[0]
    for h in range(kv // HEAD):
        at = slice(h * HEAD, (h + 1) * HEAD)
        k_out[:, at] = rotate(acc[:, at], cos_ref[...], sin_ref[...]).astype(jnp.bfloat16)
    v_out[...] = acc[:, kv:2 * kv].astype(jnp.bfloat16)

    def finish(t, carry):
        def line(d, zz):
            if ny > 1:
                for k in (1, 0):
                    y_move(zz, k).wait_send()

            @pl.when(t > 0)
            def _():
                x_move(zz, False).wait_send()

            for k in every:
                c_move(zz, False, k).wait_send()
            if ny > 1:
                x_move(zz, True).wait_send()
                for k in every:
                    c_move(zz, True, k).wait_send()

        def forward(d, zz):
            @pl.when((z + d >= 0) & (z + d < nz))
            def _():
                for k in (1, 0):
                    z_move(d, zz, k).wait_send()
                if ny > 1:
                    for other_y in (False, True):
                        b_move(d, zz, other_y).wait_send()

        blocks(t, 0, line)
        blocks(t, 1, forward)
        return carry

    @pl.when(up)
    def _():
        for k in (1, 0):
            z_move(1, z, k).wait_send()
        if ny > 1:
            for other_y in (False, True):
                b_move(1, z, other_y).wait_send()

    @pl.when(down)
    def _():
        for k in (1, 0):
            z_move(-1, z, k).wait_send()
        if ny > 1:
            for other_y in (False, True):
                b_move(-1, z, other_y).wait_send()

    if ny > 1:
        y_move(z, 3).wait_send()

    lax.fori_loop(0, nz, finish, 0)

    def drain(s, carry):
        pltpu.make_async_copy(buf.at[s, kv_rows:total, :], e_out.at[s], esem.at[s]).wait()
        return carry

    lax.fori_loop(0, buf.shape[0], drain, 0)


def steps_kernel(
    length_ref, noise_ref, input_ref, temb_ref, gain_ref, e_ref, final_ref, outw_ref, k_ref, v_ref, cos_ref, sin_ref,
    o_ref, state, keys, values, mixed,
):
    n, e3, width = e_ref.shape
    e_rows = e3 // 3
    span = noise_ref.shape[2]
    prefix, kv = k_ref.shape
    heads, kv_heads = width // HEAD, kv // HEAD
    ratio = heads // kv_heads
    length = length_ref[0]
    state[...] = jnp.zeros_like(state)
    state[:, 0:span] = noise_ref[0]
    keys[0:prefix, :] = k_ref[...]
    values[0:prefix, :] = v_ref[...]
    cosine = cos_ref[pl.ds(length, ROWS), :]
    sine = sin_ref[pl.ds(length, ROWS), :]
    at = lax.broadcasted_iota(jnp.int32, (ratio * ROWS, prefix + ROWS), 1)
    valid = (at < length) | ((at >= prefix) & (at < prefix + span))

    def weight(i):
        return e_ref[:, i * e_rows:(i + 1) * e_rows, :].reshape(n * e_rows, width)

    def step(k, carry):
        hidden = lax.dot_general(
            state[...], input_ref[...], (((0,), (0,)), ((), ())),
            precision=lax.Precision.HIGHEST, preferred_element_type=jnp.float32,
        )
        hidden = hidden + temb_ref[pl.ds(k, 1), :]
        normed = normalize(hidden, gain_ref[...]).astype(jnp.bfloat16)
        raw = jnp.dot(normed, weight(1), preferred_element_type=jnp.float32)
        for h in range(kv_heads):
            cut = slice(h * HEAD, (h + 1) * HEAD)
            keys[prefix:, cut] = rotate(raw[:, cut], cosine, sine).astype(jnp.bfloat16)
        values[prefix:, :] = raw[:, kv:].astype(jnp.bfloat16)
        raw = jnp.dot(normed, weight(0), preferred_element_type=jnp.float32)
        for h in range(kv_heads):
            cut = slice(h * HEAD, (h + 1) * HEAD)
            queries = jnp.concatenate(
                [
                    (rotate(raw[:, j * HEAD:(j + 1) * HEAD], cosine, sine) * HEAD ** (-0.5)).astype(jnp.bfloat16)
                    for j in range(h * ratio, (h + 1) * ratio)
                ],
                0,
            )
            scores = lax.dot_general(queries, keys[:, cut], (((1,), (1,)), ((), ())), preferred_element_type=jnp.float32)
            scores = jnp.where(valid, scores, -1e30)
            weights = jnp.exp(scores - jnp.max(scores, -1, keepdims=True))
            probs = (weights / jnp.sum(weights, -1, keepdims=True)).astype(jnp.bfloat16)
            out = jnp.dot(probs, values[:, cut], preferred_element_type=jnp.float32).astype(jnp.bfloat16)
            for j in range(ratio):
                mixed[:, (h * ratio + j) * HEAD:(h * ratio + j + 1) * HEAD] = out[j * ROWS:(j + 1) * ROWS]
        hidden = hidden + jnp.dot(mixed[...], weight(2), preferred_element_type=jnp.float32)
        normed = normalize(hidden, final_ref[...]).astype(jnp.bfloat16)
        velocity = lax.dot_general(outw_ref[...], normed, (((1,), (1,)), ((), ())), preferred_element_type=jnp.float32)
        state[...] = state[...] - velocity / STEPS
        return carry

    lax.fori_loop(0, STEPS, step, 0)
    o_ref[0] = state[:, 0:span]


def shards(
    nz, ny,
    prefix_hidden, prefix_lengths, action_noise, prefix_gain, key_weight, value_weight, input_weight, expert_gain,
    expert_query, expert_key, expert_value, expert_output, final_gain, output_weight,
):
    n = nz * ny * 2
    prefix, width = prefix_hidden.shape[1:]
    kv_rows, kv = key_weight.shape
    e_rows, e_width = expert_query.shape
    total = kv_rows + 3 * e_rows
    span, dim = action_noise.shape[1:]
    cosine, sine = rope_tables(prefix + ROWS + 8)
    vmem, hbm = pl.BlockSpec(memory_space=pltpu.VMEM), pl.BlockSpec(memory_space=pl.ANY)
    bf16, f32 = jnp.bfloat16, jnp.float32
    dma = pltpu.SemaphoreType.DMA
    k_cache, v_cache, expert = pl.pallas_call(
        functools.partial(gather_kernel, nz, ny),
        out_shape=(
            jax.ShapeDtypeStruct((prefix, kv), bf16),
            jax.ShapeDtypeStruct((prefix, kv), bf16),
            jax.ShapeDtypeStruct((n, 3 * e_rows, e_width), bf16),
        ),
        in_specs=[hbm] * 7 + [vmem] * 3,
        out_specs=(vmem, vmem, hbm),
        scratch_shapes=[
            pltpu.VMEM((n, total, 2 * kv), bf16),
            pltpu.VMEM((prefix, width), bf16),
            pltpu.VMEM((n, prefix, kv_rows), bf16),
            pltpu.VMEM((prefix, 2 * kv), f32),
            dma((6,)),
            dma,
            dma((n, 4)),
            dma((2, nz, 4)),
            dma((nz, 3)),
            dma((2, nz)),
            dma((ny * nz, 4)),
            dma((n,)),
        ],
        compiler_params=pltpu.CompilerParams(collective_id=0, has_side_effects=True, vmem_limit_bytes=60 * 2 ** 20),
        name="gather",
    )(
        key_weight, value_weight, expert_query, expert_key, expert_value, expert_output,
        prefix_hidden, prefix_gain.reshape(1, -1), jnp.asarray(cosine[:prefix]), jnp.asarray(sine[:prefix]),
    )
    actions = pl.pallas_call(
        steps_kernel,
        out_shape=jax.ShapeDtypeStruct((1, dim, span), f32),
        in_specs=[pl.BlockSpec(memory_space=pltpu.SMEM)] + [vmem] * 11,
        out_specs=vmem,
        scratch_shapes=[
            pltpu.VMEM((dim, ROWS), f32),
            pltpu.VMEM((prefix + ROWS, kv), bf16),
            pltpu.VMEM((prefix + ROWS, kv), bf16),
            pltpu.VMEM((ROWS, e_width), bf16),
        ],
        name="steps",
    )(
        prefix_lengths, action_noise.transpose(0, 2, 1), input_weight, jnp.asarray(time_embeddings(e_width)), expert_gain.reshape(1, -1),
        expert, final_gain.reshape(1, -1), output_weight.T, k_cache, v_cache, jnp.asarray(cosine), jnp.asarray(sine),
    )
    return actions.transpose(0, 2, 1)


def solution(mesh):
    n = mesh.shape["wide"]
    column = mesh.devices[0] if mesh.axis_names[0] == "groups" else mesh.devices[:, 0]
    ny = len({d.coords[1] for d in column.flat}) if all(hasattr(d, "coords") for d in column.flat) else 1
    nz = n // (2 * ny)
    placed = (
        P(("groups", "wide"), None, None),
        P(("groups", "wide")),
        P(("groups", "wide"), None, None),
        P(),
        P("wide", None),
        P("wide", None),
        P(),
        P(),
        P("wide", None),
        P("wide", None),
        P("wide", None),
        P("wide", None),
        P(),
        P(),
    )
    return jax.shard_map(
        functools.partial(shards, nz, ny),
        mesh=mesh,
        in_specs=placed,
        out_specs=P(("groups", "wide"), None, None),
        check_vma=False,
    )
```

```python
import functools

import jax
import jax.numpy as jnp
import numpy as np
from jax import lax
from jax.experimental import pallas as pl
from jax.experimental.pallas import tpu as pltpu
from jax.sharding import PartitionSpec as P

HEAD = 128
STEPS = 4
ROWS = 64

rope_base = 1000000.0
norm_eps = 1e-06


def rope_tables(rows):
    half = HEAD // 2
    inv = (np.float32(rope_base) ** (-np.arange(half, dtype=np.float32) * np.float32(2.0) / np.float32(HEAD))).astype(np.float32)
    angles = np.arange(rows, dtype=np.float32)[:, None] * inv[None, :]
    cosine, sine = np.cos(angles), np.sin(angles)
    return (
        np.concatenate([cosine, cosine], 1).astype(np.float32),
        np.concatenate([-sine, sine], 1).astype(np.float32),
    )


def time_embeddings(width):
    half = width // 2
    fraction = np.arange(half, dtype=np.float32) / np.float32(half - 1)
    period = np.float32(0.004) * np.float32(4.0 / 0.004) ** fraction
    rows = []
    for k in range(STEPS):
        angles = np.float32((1.0 - k / STEPS) * 2.0 * np.pi) / period
        rows.append(np.concatenate([np.sin(angles), np.cos(angles)]))
    return np.stack(rows).astype(np.float32)


def normalize(values, gain):
    mean_square = jnp.mean(values * values, axis=-1, keepdims=True)
    return values * lax.rsqrt(mean_square + norm_eps) * gain


def rotate(values, cosine, sine):
    return values * cosine + pltpu.roll(values, HEAD // 2, 1) * sine


def share(total, ny):
    if ny == 1:
        return (total * 11 // 32 + 8) // 16 * 16, 0
    return (total * 13 // 44 + 8) // 16 * 16, (total * 3 // 22 + 8) // 16 * 16


def gather_kernel(
    nz, ny,
    key_ref, value_ref, query_ref, akey_ref, avalue_ref, out_ref, hidden_ref, gain_ref, cos_ref, sin_ref,
    k_out, v_out, e_out,
    buf, hid, normed, acc,
    own_sem, hid_sem, recv, zsend, ysend, xsend, csend, esem,
):
    kv_rows, kv = key_ref.shape
    e_rows, total = query_ref.shape[0], buf.shape[1]
    r1, rb = share(total, ny)
    r0 = total - 2 * r1 - rb
    g, w = lax.axis_index("groups"), lax.axis_index("wide")
    c, y, z = w % 2, (w // 2) % ny, w // (2 * ny)
    parity = g % 2

    def shard(zz, other_y, cc):
        yy = 1 - y if other_y else y
        return (zz * ny + yy) * 2 + cc

    def piece(k):
        if k == 0:
            return 0, r0, 0
        if k == 3:
            return r0, rb, 3
        which = parity if k == 1 else 1 - parity
        return pl.multiple_of(r0 + rb + which * r1, 16), r1, 1 + which

    core = {"wide": w + 1 - 2 * c}
    across = {"groups": g + 1 - 2 * parity}
    beside = {"wide": w + 2 - 4 * y} if ny > 1 else None

    def move(s, k, send, target):
        start, size, a = piece(k)
        part = buf.at[s, pl.ds(start, size), :]
        return pltpu.make_async_remote_copy(
            src_ref=part, dst_ref=part, send_sem=send, recv_sem=recv.at[s, a],
            device_id=target, device_id_type=pl.DeviceIdType.MESH,
        )

    def arrived(s, k):
        move(s, k, csend.at[0, 0], core).wait_recv()

    up, down = z + 1 < nz, z > 0
    every = (1, 0, 2, 3) if ny > 1 else (1, 0, 2)

    def z_move(d, zz, k):
        return move(shard(zz, False, c), k, zsend.at[(d + 1) // 2, zz, k], {"wide": w + d * 2 * ny})

    def b_move(d, zz, other_y):
        return move(shard(zz, other_y, c), 3, zsend.at[(d + 1) // 2, zz, 2 + other_y], {"wide": w + d * 2 * ny})

    def y_move(zz, k):
        return move(shard(zz, False, c), k, ysend.at[zz, min(k, 2)], beside)

    def x_move(zz, other_y):
        return move(shard(zz, other_y, c), 1, xsend.at[int(other_y), zz], across)

    def c_move(zz, other_y, k):
        return move(shard(zz, other_y, c), k, csend.at[int(other_y) * nz + zz, k], core)

    own = [
        (key_ref, buf.at[w, 0:kv_rows, 0:kv]),
        (value_ref, buf.at[w, 0:kv_rows, kv:2 * kv]),
        (query_ref, buf.at[w, kv_rows:kv_rows + e_rows, :]),
        (akey_ref, buf.at[w, kv_rows + e_rows:kv_rows + 2 * e_rows, 0:kv]),
        (avalue_ref, buf.at[w, kv_rows + e_rows:kv_rows + 2 * e_rows, kv:2 * kv]),
        (out_ref, buf.at[w, kv_rows + 2 * e_rows:total, :]),
    ]
    copies = [pltpu.make_async_copy(a, b, own_sem.at[i]) for i, (a, b) in enumerate(own)]
    for copy in copies:
        copy.start()
    hid_copy = pltpu.make_async_copy(hidden_ref.at[0], hid, hid_sem)
    hid_copy.start()

    barrier = pltpu.get_barrier_semaphore()

    def greet(target):
        pl.semaphore_signal(barrier, inc=1, device_id=target, device_id_type=pl.DeviceIdType.MESH)

    greet(core)
    greet(across)
    if ny > 1:
        greet(beside)

    @pl.when(up)
    def _():
        greet({"wide": w + 2 * ny})

    @pl.when(down)
    def _():
        greet({"wide": w - 2 * ny})

    pl.semaphore_wait(barrier, 2 + (ny > 1) + up.astype(jnp.int32) + down.astype(jnp.int32))
    for copy in copies:
        copy.wait()

    for k in (1, 0):
        @pl.when(up)
        def _():
            z_move(1, z, k).start()

        @pl.when(down)
        def _():
            z_move(-1, z, k).start()

        if ny > 1:
            y_move(z, k).start()
    if ny > 1:
        y_move(z, 3).start()
    for k in every:
        c_move(z, False, k).start()

    hid_copy.wait()
    width = hid.shape[1]
    squares = jnp.zeros((hid.shape[0], HEAD), jnp.float32)

    def square(j, squares):
        part = hid[:, pl.ds(pl.multiple_of(j * HEAD, HEAD), HEAD)].astype(jnp.float32)
        return squares + part * part

    squares = lax.fori_loop(0, width // HEAD, square, squares)
    scale = lax.rsqrt(jnp.sum(squares, -1, keepdims=True) / width + norm_eps)
    wide_scale = jnp.broadcast_to(scale, (hid.shape[0], HEAD))
    per = kv_rows // HEAD

    def norm_part(j, carry):
        for i in range(per):
            at = pl.ds(pl.multiple_of((j * per + i) * HEAD, HEAD), HEAD)
            part = hid[:, at].astype(jnp.float32) * wide_scale * gain_ref[:, at]
            normed[j, :, i * HEAD:(i + 1) * HEAD] = part.astype(jnp.bfloat16)
        return carry

    lax.fori_loop(0, width // kv_rows, norm_part, 0)
    acc[...] = jnp.zeros_like(acc)

    def blocks(t, first, body):
        for d in (1, -1):
            zz = z - d * t
            ok = (zz >= 0) & (zz < nz) & (t >= first) & (t < nz)
            if d == -1:
                ok = ok & (t > 0)

            @pl.when(ok)
            def _():
                body(d, zz)

    def slot(j, first, body):
        paired = jnp.minimum(z, nz - 1 - z)
        t = jnp.where(j <= 2 * paired, (j + 1) // 2, j - paired)
        below = jnp.where(j <= 2 * paired, j % 2, (z > nz - 1 - z).astype(jnp.int32))
        zz = z + t - 2 * below * t

        @pl.when((j >= first) & (j < nz))
        def _():
            body(zz)

    def consume(zz, mine):
        def use(yy, carry):
            s = (zz * ny + (y + yy) % ny) * 2 + (c + mine) % 2
            if mine:
                for k in every:
                    arrived(s, k)
            pltpu.make_async_copy(buf.at[s, kv_rows:total, :], e_out.at[s], esem.at[s]).start()
            acc[...] += jnp.dot(normed[s], buf[s, 0:kv_rows, :], preferred_element_type=jnp.float32)
            return carry

        lax.fori_loop(0, ny, use, 0)

    def ours(zz):
        consume(zz, 0)

    def theirs(zz):
        consume(zz, 1)

    def step(i, carry):
        for k in (1, 0):
            def line(d, zz, k=k):
                arrived(shard(zz, False, c), k)

                @pl.when((z + d >= 0) & (z + d < nz))
                def _():
                    z_move(d, zz, k).start()

                if k == 1:
                    x_move(zz, False).start()
                if ny > 1:
                    if d == 1:
                        y_move(zz, k).start()
                    else:
                        @pl.when((z - i >= 0) == (k == 0))
                        def _():
                            y_move(zz, 1).start()

                        if k == 0:
                            y_move(zz, 0).start()
                c_move(zz, False, k).start()

            blocks(i, 1, line)
        def side(k):
            def body(zz):
                arrived(shard(zz, True, c), k)
                if k == 1:
                    x_move(zz, True).start()
                c_move(zz, True, k).start()

            slot(i - 1, 0, body)

        def both(d, zz):
            for other_y in (False, True):
                arrived(shard(zz, other_y, c), 3)

                @pl.when((z + d >= 0) & (z + d < nz))
                def _():
                    b_move(d, zz, other_y).start()

                c_move(zz, other_y, 3).start()

        if ny > 1:
            side(1)
        pl.when(i == nz + 1)(lambda: slot(i - 3, 0, theirs))
        if ny > 1:
            @pl.when(i == 2)
            def _():
                arrived(shard(z, True, c), 3)
                for other_y in (False, True):
                    @pl.when(up)
                    def _():
                        b_move(1, z, other_y).start()

                    @pl.when(down)
                    def _():
                        b_move(-1, z, other_y).start()

                c_move(z, True, 3).start()

            blocks(i - 2, 1, both)
            side(0)
        for other_y in ((False, True) if ny > 1 else (False,)):
            def over(zz, other_y=other_y):
                arrived(shard(zz, other_y, c), 2)
                c_move(zz, other_y, 2).start()

            slot(i - 2, 0 if other_y else 1, over)

        pl.when(i != nz + 1)(lambda: slot(i - 3, 0, theirs))
        slot(i - 2, 0, ours)
        return carry

    lax.fori_loop(0, nz + 3, step, 0)

    rows = acc.shape[0]
    for h in range(kv // HEAD):
        at = slice(h * HEAD, (h + 1) * HEAD)
        k_out[:, at] = rotate(acc[:, at], cos_ref[...], sin_ref[...]).astype(jnp.bfloat16)
    v_out[...] = acc[:, kv:2 * kv].astype(jnp.bfloat16)

    def finish(t, carry):
        def line(d, zz):
            if ny > 1:
                for k in (1, 0):
                    y_move(zz, k).wait_send()

            @pl.when(t > 0)
            def _():
                x_move(zz, False).wait_send()

            for k in every:
                c_move(zz, False, k).wait_send()
            if ny > 1:
                x_move(zz, True).wait_send()
                for k in every:
                    c_move(zz, True, k).wait_send()

        def forward(d, zz):
            @pl.when((z + d >= 0) & (z + d < nz))
            def _():
                for k in (1, 0):
                    z_move(d, zz, k).wait_send()
                if ny > 1:
                    for other_y in (False, True):
                        b_move(d, zz, other_y).wait_send()

        blocks(t, 0, line)
        blocks(t, 1, forward)
        return carry

    @pl.when(up)
    def _():
        for k in (1, 0):
            z_move(1, z, k).wait_send()
        if ny > 1:
            for other_y in (False, True):
                b_move(1, z, other_y).wait_send()

    @pl.when(down)
    def _():
        for k in (1, 0):
            z_move(-1, z, k).wait_send()
        if ny > 1:
            for other_y in (False, True):
                b_move(-1, z, other_y).wait_send()

    if ny > 1:
        y_move(z, 3).wait_send()

    lax.fori_loop(0, nz, finish, 0)

    def drain(s, carry):
        pltpu.make_async_copy(buf.at[s, kv_rows:total, :], e_out.at[s], esem.at[s]).wait()
        return carry

    lax.fori_loop(0, buf.shape[0], drain, 0)


def steps_kernel(
    length_ref, noise_ref, input_ref, temb_ref, gain_ref, e_ref, final_ref, outw_ref, k_ref, v_ref, cos_ref, sin_ref,
    o_ref, state, keys, values, mixed,
):
    n, e3, width = e_ref.shape
    e_rows = e3 // 3
    span = noise_ref.shape[2]
    prefix, kv = k_ref.shape
    heads, kv_heads = width // HEAD, kv // HEAD
    ratio = heads // kv_heads
    length = length_ref[0]
    state[...] = jnp.zeros_like(state)
    state[:, 0:span] = noise_ref[0]
    keys[0:prefix, :] = k_ref[...]
    values[0:prefix, :] = v_ref[...]
    cosine = cos_ref[pl.ds(length, ROWS), :]
    sine = sin_ref[pl.ds(length, ROWS), :]
    at = lax.broadcasted_iota(jnp.int32, (ratio * ROWS, prefix + ROWS), 1)
    valid = (at < length) | ((at >= prefix) & (at < prefix + span))

    def weight(i):
        return e_ref[:, i * e_rows:(i + 1) * e_rows, :].reshape(n * e_rows, width)

    def step(k, carry):
        hidden = lax.dot_general(
            state[...], input_ref[...], (((0,), (0,)), ((), ())),
            precision=lax.Precision.HIGHEST, preferred_element_type=jnp.float32,
        )
        hidden = hidden + temb_ref[pl.ds(k, 1), :]
        normed = normalize(hidden, gain_ref[...]).astype(jnp.bfloat16)
        raw = jnp.dot(normed, weight(1), preferred_element_type=jnp.float32)
        for h in range(kv_heads):
            cut = slice(h * HEAD, (h + 1) * HEAD)
            keys[prefix:, cut] = rotate(raw[:, cut], cosine, sine).astype(jnp.bfloat16)
        values[prefix:, :] = raw[:, kv:].astype(jnp.bfloat16)
        raw = jnp.dot(normed, weight(0), preferred_element_type=jnp.float32)
        for h in range(kv_heads):
            cut = slice(h * HEAD, (h + 1) * HEAD)
            queries = jnp.concatenate(
                [
                    (rotate(raw[:, j * HEAD:(j + 1) * HEAD], cosine, sine) * HEAD ** (-0.5)).astype(jnp.bfloat16)
                    for j in range(h * ratio, (h + 1) * ratio)
                ],
                0,
            )
            scores = lax.dot_general(queries, keys[:, cut], (((1,), (1,)), ((), ())), preferred_element_type=jnp.float32)
            scores = jnp.where(valid, scores, -1e30)
            weights = jnp.exp(scores - jnp.max(scores, -1, keepdims=True))
            probs = (weights / jnp.sum(weights, -1, keepdims=True)).astype(jnp.bfloat16)
            out = jnp.dot(probs, values[:, cut], preferred_element_type=jnp.float32).astype(jnp.bfloat16)
            for j in range(ratio):
                mixed[:, (h * ratio + j) * HEAD:(h * ratio + j + 1) * HEAD] = out[j * ROWS:(j + 1) * ROWS]
        hidden = hidden + jnp.dot(mixed[...], weight(2), preferred_element_type=jnp.float32)
        normed = normalize(hidden, final_ref[...]).astype(jnp.bfloat16)
        velocity = lax.dot_general(outw_ref[...], normed, (((1,), (1,)), ((), ())), preferred_element_type=jnp.float32)
        state[...] = state[...] - velocity / STEPS
        return carry

    lax.fori_loop(0, STEPS, step, 0)
    o_ref[0] = state[:, 0:span]


def shards(
    nz, ny,
    prefix_hidden, prefix_lengths, action_noise, prefix_gain, key_weight, value_weight, input_weight, expert_gain,
    expert_query, expert_key, expert_value, expert_output, final_gain, output_weight,
):
    n = nz * ny * 2
    prefix, width = prefix_hidden.shape[1:]
    kv_rows, kv = key_weight.shape
    e_rows, e_width = expert_query.shape
    total = kv_rows + 3 * e_rows
    span, dim = action_noise.shape[1:]
    cosine, sine = rope_tables(prefix + ROWS + 8)
    vmem, hbm = pl.BlockSpec(memory_space=pltpu.VMEM), pl.BlockSpec(memory_space=pl.ANY)
    bf16, f32 = jnp.bfloat16, jnp.float32
    dma = pltpu.SemaphoreType.DMA
    k_cache, v_cache, expert = pl.pallas_call(
        functools.partial(gather_kernel, nz, ny),
        out_shape=(
            jax.ShapeDtypeStruct((prefix, kv), bf16),
            jax.ShapeDtypeStruct((prefix, kv), bf16),
            jax.ShapeDtypeStruct((n, 3 * e_rows, e_width), bf16),
        ),
        in_specs=[hbm] * 7 + [vmem] * 3,
        out_specs=(vmem, vmem, hbm),
        scratch_shapes=[
            pltpu.VMEM((n, total, 2 * kv), bf16),
            pltpu.VMEM((prefix, width), bf16),
            pltpu.VMEM((n, prefix, kv_rows), bf16),
            pltpu.VMEM((prefix, 2 * kv), f32),
            dma((6,)),
            dma,
            dma((n, 4)),
            dma((2, nz, 4)),
            dma((nz, 3)),
            dma((2, nz)),
            dma((ny * nz, 4)),
            dma((n,)),
        ],
        compiler_params=pltpu.CompilerParams(collective_id=0, has_side_effects=True, vmem_limit_bytes=60 * 2 ** 20),
        name="gather",
    )(
        key_weight, value_weight, expert_query, expert_key, expert_value, expert_output,
        prefix_hidden, prefix_gain.reshape(1, -1), jnp.asarray(cosine[:prefix]), jnp.asarray(sine[:prefix]),
    )
    actions = pl.pallas_call(
        steps_kernel,
        out_shape=jax.ShapeDtypeStruct((1, dim, span), f32),
        in_specs=[pl.BlockSpec(memory_space=pltpu.SMEM)] + [vmem] * 11,
        out_specs=vmem,
        scratch_shapes=[
            pltpu.VMEM((dim, ROWS), f32),
            pltpu.VMEM((prefix + ROWS, kv), bf16),
            pltpu.VMEM((prefix + ROWS, kv), bf16),
            pltpu.VMEM((ROWS, e_width), bf16),
        ],
        name="steps",
    )(
        prefix_lengths, action_noise.transpose(0, 2, 1), input_weight, jnp.asarray(time_embeddings(e_width)), expert_gain.reshape(1, -1),
        expert, final_gain.reshape(1, -1), output_weight.T, k_cache, v_cache, jnp.asarray(cosine), jnp.asarray(sine),
    )
    return actions.transpose(0, 2, 1)


def solution(mesh):
    n = mesh.shape["wide"]
    column = mesh.devices[0] if mesh.axis_names[0] == "groups" else mesh.devices[:, 0]
    ny = len({d.coords[1] for d in column.flat}) if all(hasattr(d, "coords") for d in column.flat) else 1
    nz = n // (2 * ny)
    placed = (
        P(("groups", "wide"), None, None),
        P(("groups", "wide")),
        P(("groups", "wide"), None, None),
        P(),
        P("wide", None),
        P("wide", None),
        P(),
        P(),
        P("wide", None),
        P("wide", None),
        P("wide", None),
        P("wide", None),
        P(),
        P(),
    )
    return jax.shard_map(
        functools.partial(shards, nz, ny),
        mesh=mesh,
        in_specs=placed,
        out_specs=P(("groups", "wide"), None, None),
        check_vma=False,
    )
```
